32 devices in a mesh: grp: 2 (over y), kvp: 4 (over x, core), tp: 4 (over z).
Axes of the slice: x: 2, y: 2, z: 4, core: 2. Of those that a mesh axis runs over, the one named last changes fastest.
Arguments:
- normed: bfloat16 [512, 6144], P('grp', 'kvp'), parts along dimension 0, may hold values from -6 to 6
- w_query: bfloat16 [6144, 6144], P('kvp', 'tp'), may hold values from -0.078125 to 0.078125
- w_key: bfloat16 [6144, 1024], P('kvp', 'tp'), may hold values from -0.078125 to 0.078125
- w_value: bfloat16 [6144, 1024], P('kvp', 'tp'), may hold values from -0.078125 to 0.078125
- w_out: bfloat16 [6144, 6144], P('tp', 'kvp'), may hold values from -0.078125 to 0.078125
- key_cache: bfloat16 [8, 1024, 128, 128], P('tp', ('grp', 'kvp')), parts along dimension 1, may hold values from -128 to 128
- value_cache: bfloat16 [8, 1024, 128, 128], P('tp', ('grp', 'kvp')), parts along dimension 1, may hold values from -6 to 6
- lengths: int32 [512], P('grp'), parts along dimension 0, may hold values from 1 to 12288, as said below
- page_table: int32 [512, 96], P('grp'), parts along dimension 0, may hold values from -1 to 511, as said below
Outputs:
- attended: bfloat16 [512, 6144], P(('grp', 'tp'), 'kvp'), parts along dimension 0
The draws below stay inside these ranges and needn't reach their ends.
There are 2 independent parts, one for each index of `grp`. The reference program is written for one: setup_inputs(seed, part) draws one part's arguments, and reference() takes and returns one part's arrays. A program takes and returns all parts, laid end to end along the dimension named above; an argument that names none is the same for every part. Nothing has to cross between parts.
Inputs may be any that keep to these rules, and one draw needn't show every extreme that they name: `lengths`: every request has at least one cached token; the longest request fills all 96 entries of its page table. `page_table`: entry [b, j] is a page index exactly when j < ceil(lengths[b] / 128), else -1; no page is named twice. Index kvp = i holds pages i * 128 to (i + 1) * 128 - 1; the pages in use are spread unevenly over kvp.
All inputs are finite; a program needn't handle non-finite values.
Results may differ from the reference program's by a relative error of at most 0.012.
Values may be sent and summed in bfloat16 or wider, within the bound.
No kernel may reach another device: no remote copies, remote signals or barrier semaphores. Data moves between devices by JAX's collectives and lax.ppermute only.
A program may use at most 64 MiB of HBM per device.

```python
import jax
import jax.numpy as jnp
from jax import lax

D = 6144
HEADS = 48
KV_HEADS = 8
HEAD_DIM = 128
BATCH = 256
PAGES_DEV = 128
PAGE = 128
SLOTS = 512
USED = 384
MAXP = 96


def layout(key):
    base = jax.random.fold_in(key, 4242)
    keys = jax.random.split(base, 7)
    longest = jax.random.randint(keys[0], (), 0, BATCH)
    rows = jnp.arange(BATCH, dtype=jnp.int32)
    raw = jax.random.randint(keys[1], (BATCH,), 1, 65) * jax.random.randint(keys[2], (BATCH,), 1, 65)
    raw = jnp.where(rows == longest, 0, raw)
    spare = USED - MAXP - (BATCH - 1)
    extra = raw * spare // jnp.maximum(jnp.sum(raw), 1)
    blocks = jnp.minimum(1 + extra, MAXP)
    blocks = jnp.where(rows == longest, MAXP, blocks)
    tail = jax.random.randint(keys[3], (BATCH,), 1, PAGE + 1)
    lengths = (blocks - 1) * PAGE + tail
    lengths = jnp.where(rows == longest, MAXP * PAGE, lengths).astype(jnp.int32)
    pages = jnp.arange(SLOTS, dtype=jnp.int32)
    device = pages // PAGES_DEV
    within = pages % PAGES_DEV
    devices = SLOTS // PAGES_DEV
    bias = jax.random.randint(keys[4], (devices,), 1, 5)[device]
    tie = jax.random.permutation(keys[5], SLOTS).astype(jnp.int32)
    score = within * bias * SLOTS + tie
    order = jnp.argsort(score, stable=True).astype(jnp.int32)
    chosen = order[:USED]
    chosen = chosen[jax.random.permutation(keys[6], USED)]
    offsets = jnp.cumsum(blocks) - blocks
    column = jnp.arange(MAXP, dtype=jnp.int32)
    flat = offsets[:, None] + column[None, :]
    valid = column[None, :] < blocks[:, None]
    table = jnp.where(valid, chosen[jnp.clip(flat, 0, USED - 1)], -1).astype(jnp.int32)
    return (lengths, table)


def draw_lengths(key, part):
    return layout(key)[0]


def draw_page_table(key, part):
    return layout(key)[1]


def draw_key_cache(key, part):
    first = jax.random.fold_in(jax.random.fold_in(key, 77), 0)
    values = jnp.clip(jax.random.normal(first, (KV_HEADS, SLOTS, PAGE, HEAD_DIM), jnp.float32), -4.0, 4.0)
    return values.astype(jnp.bfloat16)


def levels(rng, shape, cuts, smallest, top_value):
    def one(dim, shards_of):
        heights = jax.random.uniform(jax.random.fold_in(jax.random.fold_in(rng, 6), dim), (shards_of,), jnp.float32, smallest / len(cuts), top_value / len(cuts))
        return jnp.repeat(jnp.exp(heights), shape[dim] // shards_of).reshape((-1,) + (1,) * (len(shape) - dim - 1))

    factor_of = one(*cuts[0])
    for cut in cuts[1:]:
        factor_of = factor_of * one(*cut)
    return factor_of


def normal_values(stream_key, dims, spread, limit, cuts=(), held_as=jnp.bfloat16):
    array = spread * jax.random.normal(stream_key, dims, jnp.float32)
    if cuts:
        array = array * levels(stream_key, dims, cuts, -0.22, 0.18)
    return jnp.clip(array, -limit, limit).astype(held_as)


def setup_inputs(seed: int = 0, part: int = 0) -> dict:
    arg_keys = jax.random.split(jax.random.key(seed), 10)
    part_keys = jax.random.split(jax.random.fold_in(arg_keys[9], part), 10)
    normed = normal_values(part_keys[0], (BATCH, D), 1.0, 6.0, ((1, 4),))
    w_query = normal_values(arg_keys[1], (D, HEADS * HEAD_DIM), D ** -0.5, 0.078125, ((0, 4), (1, 4)))
    w_key = normal_values(arg_keys[2], (D, KV_HEADS * HEAD_DIM), D ** -0.5, 0.078125, ((0, 4), (1, 4)))
    w_value = normal_values(arg_keys[3], (D, KV_HEADS * HEAD_DIM), D ** -0.5, 0.078125, ((0, 4), (1, 4)))
    w_out = normal_values(arg_keys[4], (HEADS * HEAD_DIM, D), (HEADS * HEAD_DIM) ** -0.5, 0.078125, ((0, 4), (1, 4)))
    key_cache = draw_key_cache(jax.random.fold_in(jax.random.fold_in(arg_keys[9], part), 71), part)
    value_cache = normal_values(part_keys[6], (KV_HEADS, SLOTS, PAGE, HEAD_DIM), 1.0, 6.0, ((0, 4), (1, 4)))
    lengths = draw_lengths(jax.random.fold_in(jax.random.fold_in(arg_keys[9], part), 71), part)
    page_table = draw_page_table(jax.random.fold_in(jax.random.fold_in(arg_keys[9], part), 71), part)
    return dict(normed=normed, w_query=w_query, w_key=w_key, w_value=w_value, w_out=w_out, key_cache=key_cache, value_cache=value_cache, lengths=lengths, page_table=page_table)


ROPE_BASE = 1000000.0
NEG = -1.0e30
TWO_PI_HIGH = 6.28125
TWO_PI_LOW = 0.0019353071795864769


def rotate(x, pos):
    width = x.shape[-1]
    half = width // 2
    freq = ROPE_BASE ** (-(2.0 * jnp.arange(half, dtype=jnp.float32)) / width)
    coarse = lax.optimization_barrier(freq.astype(jnp.bfloat16)).astype(jnp.float32)
    fine = freq - coarse
    pos_e = pos[..., None]
    exact = pos_e * coarse
    turns = jnp.floor(exact / TWO_PI_HIGH)
    angle = (exact - turns * TWO_PI_HIGH) - turns * TWO_PI_LOW + pos_e * fine
    cosine = jnp.cos(angle)
    sine = jnp.sin(angle)
    first = x[..., :half]
    second = x[..., half:]
    return jnp.concatenate([first * cosine - second * sine, second * cosine + first * sine], axis=-1)


def reference(normed, w_query, w_key, w_value, w_out, key_cache, value_cache, lengths, page_table):
    group = HEADS // KV_HEADS
    query = jnp.dot(normed, w_query, preferred_element_type=jnp.float32)
    key_new = jnp.dot(normed, w_key, preferred_element_type=jnp.float32)
    value_new = jnp.dot(normed, w_value, preferred_element_type=jnp.float32)
    position = lengths.astype(jnp.float32)
    q_rot = rotate(query.reshape(BATCH, KV_HEADS, group, HEAD_DIM), position[:, None, None]).astype(jnp.bfloat16)
    k_rot = rotate(key_new.reshape(BATCH, KV_HEADS, HEAD_DIM), position[:, None]).astype(jnp.bfloat16)
    v_new = value_new.reshape(BATCH, KV_HEADS, HEAD_DIM).astype(jnp.bfloat16)
    scale = HEAD_DIM ** -0.5

    def one_request(items):
        q_one, k_one, v_one, length, table = items
        index = jnp.maximum(table, 0).astype(jnp.int32)
        keys = key_cache[:, index].reshape(KV_HEADS, MAXP * PAGE, HEAD_DIM).astype(jnp.float32)
        values = value_cache[:, index].reshape(KV_HEADS, MAXP * PAGE, HEAD_DIM).astype(jnp.float32)
        valid = jnp.arange(MAXP * PAGE, dtype=jnp.int32) < length
        qf = q_one.astype(jnp.float32)
        scores = jnp.einsum('hgd,htd->hgt', qf, keys) * scale
        scores = jnp.where(valid[None, None, :], scores, NEG)
        s_new = jnp.einsum('hgd,hd->hg', qf, k_one.astype(jnp.float32)) * scale
        top = jnp.maximum(jnp.max(scores, axis=-1), s_new)
        weights = jnp.where(valid[None, None, :], jnp.exp(scores - top[..., None]), 0.0)
        w_new = jnp.exp(s_new - top)
        total = jnp.sum(weights, axis=-1) + w_new
        acc = jnp.einsum('hgt,htd->hgd', weights.astype(jnp.bfloat16).astype(jnp.float32), values)
        acc = acc + w_new[..., None] * v_one.astype(jnp.float32)[:, None, :]
        return (acc / total[..., None]).astype(jnp.bfloat16)

    head_out = lax.map(one_request, (q_rot, k_rot, v_new, lengths, page_table))
    head_out = head_out.reshape(BATCH, HEADS * HEAD_DIM)
    return jnp.dot(head_out, w_out, preferred_element_type=jnp.float32).astype(jnp.bfloat16)
```

```python
import functools

import jax
import jax.numpy as jnp
from jax import lax
from jax.experimental import pallas as pl
from jax.experimental.pallas import tpu as pltpu
from jax.sharding import PartitionSpec as P

ROPE_BASE = 1000000.0
NEG = -1e30
TWO_PI_HIGH = 6.28125
TWO_PI_LOW = 0.0019353071795864769
LANES = 128
F32 = jnp.float32
BF16 = jnp.bfloat16
VMEM_LIMIT = 56 * 1024 * 1024


def angles(pos, width):
    half = width // 2
    freq = ROPE_BASE ** (-(2.0 * jnp.arange(half, dtype=F32)) / width)
    coarse = lax.optimization_barrier(freq.astype(BF16)).astype(F32)
    fine = freq - coarse
    pos_e = pos[..., None]
    exact = pos_e * coarse
    turns = jnp.floor(exact / TWO_PI_HIGH)
    angle = exact - turns * TWO_PI_HIGH - turns * TWO_PI_LOW + pos_e * fine
    cosine = jnp.cos(angle)
    sine = jnp.sin(angle)
    return jnp.concatenate([cosine, cosine], -1), jnp.concatenate([-sine, sine], -1)


def whole_spec():
    return pl.BlockSpec(memory_space=pltpu.VMEM)


def params(**kw):
    return pltpu.CompilerParams(vmem_limit_bytes=VMEM_LIMIT, **kw)


def project_kernel(half, place, n_ref, *refs):
    count = len(refs) - 2
    other_ref, mine_ref = refs[count:]
    core = place[0]
    rows = jnp.concatenate(
        [
            n_ref[pl.ds(pl.multiple_of((1 - core) * half, half), half), :],
            n_ref[pl.ds(pl.multiple_of(core * half, half), half), :],
        ],
        axis=0,
    )
    at = 0
    for w_ref in refs[:count]:
        width = w_ref.shape[1]
        acc = jnp.dot(rows, w_ref[...], preferred_element_type=F32)
        other_ref[:, at : at + width] = acc[:half]
        mine_ref[:, at : at + width] = acc[half:]
        at += width


def project(place, normed, weights, start, width, tile):
    batch, depth = normed.shape
    half = batch // 2
    steps = width // tile
    first = start // tile
    out = jax.ShapeDtypeStruct((half, width * len(weights)), F32)
    wide = tile * len(weights)
    return pl.pallas_call(
        functools.partial(project_kernel, half),
        out_shape=(out, out),
        grid_spec=pltpu.PrefetchScalarGridSpec(
            num_scalar_prefetch=1,
            grid=(steps,),
            in_specs=[pl.BlockSpec((batch, depth), lambda i, p: (0, 0))]
            + [pl.BlockSpec((depth, tile), lambda i, p: (0, first + i)) for _ in weights],
            out_specs=[pl.BlockSpec((half, wide), lambda i, p: (0, i))] * 2,
        ),
        compiler_params=params(),
        cost_estimate=pl.CostEstimate(
            flops=2 * batch * depth * width * len(weights),
            transcendentals=0,
            bytes_accessed=2 * depth * (batch + width * len(weights)) + 8 * half * width * len(weights),
        ),
        name="project",
    )(place, normed, *weights)


def table_kernel(batch, half, pages, place, t_ref, c_ref, owner_ref, count_ref, acc_ref):
    core = place[0]
    first = place[1] * pages
    acc_ref[...] = jnp.zeros_like(acc_ref)
    slot = lax.broadcasted_iota(jnp.int32, acc_ref.shape, 0) + first

    def step(r, carry):
        ids = t_ref[pl.ds(r * 8, 8), :]
        codes = c_ref[pl.ds(r * 8, 8), :]
        total = carry
        for k in range(8):
            total = total + jnp.where(ids[k : k + 1, :] == slot, codes[k : k + 1, :], 0)
        return total

    total = lax.fori_loop(0, t_ref.shape[0] // 8, step, jnp.zeros(acc_ref.shape, jnp.int32))
    code = jnp.sum(total, axis=1, keepdims=True)
    owner = lax.shift_right_logical(code, 8) - core * half
    owner_ref[...] = jnp.where(owner < 0, owner + batch, owner)
    count_ref[...] = code & 255


def invert_table(place, page_table, lengths, pages, page, half):
    batch, blocks = page_table.shape
    left = lengths[:, None] - page * jnp.arange(blocks, dtype=jnp.int32)[None, :]
    code = jnp.arange(batch, dtype=jnp.int32)[:, None] * 256 + jnp.clip(left, 0, page)
    column = jax.ShapeDtypeStruct((pages, 1), jnp.int32)
    return pl.pallas_call(
        functools.partial(table_kernel, batch, half, pages),
        out_shape=(column, column),
        in_specs=[pl.BlockSpec(memory_space=pltpu.SMEM), whole_spec(), whole_spec()],
        out_specs=[whole_spec(), whole_spec()],
        scratch_shapes=[pltpu.VMEM((pages, LANES), jnp.int32)],
        compiler_params=params(),
        name="table",
    )(place, page_table.reshape(-1, LANES), code.reshape(-1, LANES))


def rotate_kernel(plain, *refs):
    cos_ref, sin_ref, out_ref = refs[-3:]
    parts = refs[:-3]
    cosine = cos_ref[...]
    sine = sin_ref[...]
    for at in range(0, out_ref.shape[1], LANES):
        cols = slice(at, at + LANES)
        x = parts[0][:, cols].astype(F32)
        for part in parts[1:]:
            x = x + part[:, cols].astype(F32)
        if at < plain:
            x = x * cosine + pltpu.roll(x, LANES // 2, 1) * sine
        out_ref[:, cols] = x.astype(BF16)


def rotate_sum(parts, cosine, sine, plain):
    return pl.pallas_call(
        functools.partial(rotate_kernel, plain),
        out_shape=jax.ShapeDtypeStruct(parts[0].shape, BF16),
        in_specs=[whole_spec()] * (len(parts) + 2),
        out_specs=whole_spec(),
        compiler_params=params(),
        name="rotate",
    )(*parts, cosine, sine)


def attend_kernel(group, scale, step_slots, qm_ref, qo_ref, own_ref, cnt_ref, k_ref, v_ref, mine_ref, other_ref, q_sc, o_sc, l_sc):
    pages = own_ref.shape[0]
    half = qm_ref.shape[0]
    batch = 2 * half
    step = pl.program_id(0)
    lane_row = lax.broadcasted_iota(jnp.int32, (pages, batch), 1)

    @pl.when(step == 0)
    def _():
        pick = jnp.where(own_ref[...] == lane_row, 1.0, 0.0).astype(BF16)
        q_sc[...] = jnp.dot(pick[:, :half], qm_ref[...], preferred_element_type=F32) + jnp.dot(
            pick[:, half:], qo_ref[...], preferred_element_type=F32
        )

    sub = lax.broadcasted_iota(jnp.int32, (group * 8, LANES), 0) % 8
    lane = lax.broadcasted_iota(jnp.int32, (group * 8, LANES), 1)
    lane8 = lax.broadcasted_iota(jnp.int32, (8, LANES), 1)
    for i in range(step_slots // 8):
        base = pl.multiple_of(step * step_slots + i * 8, 8)
        q = jnp.concatenate(
            [q_sc[pl.ds(base, 8), h * LANES : (h + 1) * LANES] for h in range(group)], axis=0
        ).astype(BF16)
        keys = k_ref[i * 8 : (i + 1) * 8].reshape(8 * LANES, LANES)
        values = v_ref[i * 8 : (i + 1) * 8].reshape(8 * LANES, LANES)
        raw = lax.dot_general(q, keys, (((1,), (1,)), ((), ())), preferred_element_type=F32)
        s = raw[:, :LANES]
        for k in range(1, 8):
            s = jnp.where(sub == k, raw[:, k * LANES : (k + 1) * LANES], s)
        count = jnp.concatenate([cnt_ref[pl.ds(base, 8), :]] * group, axis=0)
        valid = lane < count
        s = jnp.where(valid, s * scale, NEG)
        top = jnp.max(s, axis=1, keepdims=True)
        w = jnp.where(valid, jnp.exp(s - top), 0.0)
        total = jnp.sum(w, axis=1, keepdims=True)
        spread = jnp.concatenate([jnp.where(sub == k, w, 0.0) for k in range(8)], axis=1).astype(BF16)
        out = jnp.dot(spread, values, preferred_element_type=F32)
        some = count > 0
        safe = jnp.where(some, total, 1.0)
        out = jnp.where(some, out / safe, 0.0)
        lse = jnp.where(some, top + jnp.log(safe), NEG)
        packed = jnp.full((8, LANES), NEG, F32)
        for h in range(group):
            o_sc[pl.ds(base, 8), h * LANES : (h + 1) * LANES] = out[h * 8 : (h + 1) * 8]
            packed = jnp.where(lane8 == h, lse[h * 8 : (h + 1) * 8], packed)
        l_sc[pl.ds(base, 8), :] = packed

    @pl.when(step == pl.num_programs(0) - 1)
    def _():
        mask = (own_ref[...] == lane_row) & (cnt_ref[...] > 0)
        row_lse = []
        for h in range(group):
            cols = slice(h * LANES, (h + 1) * LANES)
            col = jnp.where(mask, l_sc[:, h : h + 1], NEG)
            top = jnp.max(col, axis=0, keepdims=True)
            e = jnp.where(mask, jnp.exp(col - top), 0.0)
            total = jnp.sum(e, axis=0, keepdims=True)
            some = total > 0.0
            safe = jnp.where(some, total, 1.0)
            w = (e / safe).astype(BF16)
            rows = lax.dot_general(
                w, o_sc[:, cols].astype(BF16), (((0,), (0,)), ((), ())), preferred_element_type=F32
            )
            mine_ref[:, cols] = rows[:half]
            other_ref[:, cols] = rows[half:]
            row_lse.append(jnp.where(some, top + jnp.log(safe), NEG))
        row_lse.append(jnp.full((LANES - group, batch), NEG, F32))
        flipped = jnp.concatenate(row_lse, axis=0).T
        mine_ref[:, group * LANES :] = flipped[:half]
        other_ref[:, group * LANES :] = flipped[half:]


def attend(q_mine, q_other, owner, count, key_cache, value_cache, head, scale):
    half, width = q_mine.shape
    group = width // LANES
    pages, page, dim = key_cache.shape[1:]
    step_slots = 16 if pages % 16 == 0 else 8
    out = jax.ShapeDtypeStruct((half, width + LANES), F32)
    fixed = lambda shape: pl.BlockSpec(shape, lambda i: (0,) * len(shape))
    cache = pl.BlockSpec((None, step_slots, page, dim), lambda i: (head, i, 0, 0))
    return pl.pallas_call(
        functools.partial(attend_kernel, group, scale, step_slots),
        out_shape=(out, out),
        grid=(pages // step_slots,),
        in_specs=[fixed((half, width)), fixed((half, width)), fixed((pages, 1)), fixed((pages, 1)), cache, cache],
        out_specs=[fixed((half, width + LANES))] * 2,
        scratch_shapes=[
            pltpu.VMEM((pages, width), F32),
            pltpu.VMEM((pages, width), F32),
            pltpu.VMEM((pages, LANES), F32),
        ],
        compiler_params=params(),
        cost_estimate=pl.CostEstimate(
            flops=4 * pages * page * dim * group * 8,
            transcendentals=pages * page * group,
            bytes_accessed=4 * pages * page * dim,
        ),
        name="attend",
    )(q_mine, q_other, owner, count, key_cache, value_cache)


def pair_kernel(group, a_ref, b_ref, out_ref):
    la = a_ref[:, group * LANES :]
    lb = b_ref[:, group * LANES :]
    top = jnp.maximum(la, lb)
    wa = jnp.exp(la - top)
    wb = jnp.exp(lb - top)
    total = wa + wb
    wa = wa / total
    wb = wb / total
    for h in range(group):
        cols = slice(h * LANES, (h + 1) * LANES)
        out_ref[:, cols] = (wa[:, h : h + 1] * a_ref[:, cols] + wb[:, h : h + 1] * b_ref[:, cols]).astype(BF16)
    lse = top + jnp.log(total)
    lane = lax.broadcasted_iota(jnp.int32, lse.shape, 1)
    high = lse.astype(BF16).astype(F32)
    rest = lse - high
    middle = rest.astype(BF16).astype(F32)
    low = rest - middle
    packed = jnp.where(lane < 8, high, 0.0)
    packed = jnp.where((lane >= 8) & (lane < 16), pltpu.roll(middle, 8, 1), packed)
    packed = jnp.where((lane >= 16) & (lane < 24), pltpu.roll(low, 16, 1), packed)
    out_ref[:, group * LANES :] = packed.astype(BF16)


def pair_merge(a, b, group):
    return pl.pallas_call(
        functools.partial(pair_kernel, group),
        out_shape=jax.ShapeDtypeStruct(a.shape, BF16),
        in_specs=[whole_spec()] * 2,
        out_specs=whole_spec(),
        compiler_params=params(),
        name="pair",
    )(a, b)


def finish_kernel(group, scale, head, kv_local, *refs):
    q_ref, kv_ref, out_ref = refs[-3:]
    parts = refs[:-3]
    keys = kv_ref[:, head * LANES : (head + 1) * LANES].astype(F32)
    values = kv_ref[:, (kv_local + head) * LANES : (kv_local + head + 1) * LANES].astype(F32)
    lses = []
    for part in parts:
        x = part[:, group * LANES :].astype(F32)
        lses.append(x + pltpu.roll(x, LANES - 8, 1) + pltpu.roll(x, LANES - 16, 1))
    for h in range(group):
        cols = slice(h * LANES, (h + 1) * LANES)
        s_new = jnp.sum(q_ref[:, cols].astype(F32) * keys, axis=1, keepdims=True) * scale
        top = s_new
        for lse in lses:
            top = jnp.maximum(top, lse[:, h : h + 1])
        w_new = jnp.exp(s_new - top)
        total = w_new
        acc = w_new * values
        for part, lse in zip(parts, lses):
            w = jnp.exp(lse[:, h : h + 1] - top)
            total = total + w
            acc = acc + w * part[:, cols].astype(F32)
        out_ref[:, cols] = (acc / total).astype(BF16)


def finish(parts, q_mine, kv_rows, head, kv_local, scale):
    group = q_mine.shape[1] // LANES
    return pl.pallas_call(
        functools.partial(finish_kernel, group, scale, head, kv_local),
        out_shape=jax.ShapeDtypeStruct(q_mine.shape, BF16),
        in_specs=[whole_spec()] * (len(parts) + 2),
        out_specs=whole_spec(),
        compiler_params=params(),
        name="finish",
    )(*parts, q_mine, kv_rows)


def output_kernel(rows, heads, place, *refs):
    ins = refs[: 2 * heads]
    w_ref = refs[2 * heads]
    outs = refs[2 * heads + 1 : -1]
    x_sc = refs[-1]
    batch = x_sc.shape[0]
    half = batch // 2
    core = place[0]
    me = place[2]
    width = ins[0].shape[1]
    ways = batch // rows

    @pl.when(pl.program_id(0) == 0)
    def _():
        for h in range(heads):
            cols = slice(h * width, (h + 1) * width)
            x_sc[pl.ds(pl.multiple_of(core * half, half), half), cols] = ins[2 * h][...]
            x_sc[pl.ds(pl.multiple_of((1 - core) * half, half), half), cols] = ins[2 * h + 1][...]

    x = jnp.concatenate(
        [x_sc[pl.ds(pl.multiple_of(lax.rem(me + k, ways) * rows, rows), rows), :] for k in range(ways)], axis=0
    )
    acc = jnp.dot(x, w_ref[...], preferred_element_type=F32)
    for k, out in enumerate(outs):
        out[...] = acc[k * rows : (k + 1) * rows].astype(out.dtype)


def project_out(place, pieces, w_out, rows):
    heads = len(pieces)
    half, width = pieces[0][0].shape
    batch = 2 * half
    depth, columns = w_out.shape
    tile = 256 if columns % 256 == 0 else LANES
    ways = batch // rows
    fixed = lambda shape: pl.BlockSpec(shape, lambda i, p: (0,) * len(shape))
    return pl.pallas_call(
        functools.partial(output_kernel, rows, heads),
        out_shape=[jax.ShapeDtypeStruct((rows, columns), F32 if k == 0 else BF16) for k in range(ways)],
        grid_spec=pltpu.PrefetchScalarGridSpec(
            num_scalar_prefetch=1,
            grid=(columns // tile,),
            in_specs=[fixed((half, width))] * (2 * heads) + [pl.BlockSpec((depth, tile), lambda i, p: (0, i))],
            out_specs=[pl.BlockSpec((rows, tile), lambda i, p: (0, i))] * ways,
            scratch_shapes=[pltpu.VMEM((batch, depth), BF16)],
        ),
        compiler_params=params(),
        cost_estimate=pl.CostEstimate(
            flops=2 * batch * depth * columns, transcendentals=0, bytes_accessed=2 * depth * columns + 2 * batch * columns
        ),
        name="project_out",
    )(place, *[x for piece in pieces for x in piece], w_out)


def body(normed, w_query, w_key, w_value, w_out, key_cache, value_cache, lengths, page_table):
    batch = normed.shape[0]
    kv_local, pages, page, head_dim = key_cache.shape
    group = w_query.shape[1] // (kv_local * head_dim)
    width = group * head_dim
    scale = head_dim ** (-0.5)
    spread = lax.axis_size("kvp")
    ways = lax.axis_size("tp")
    chips = spread // 2
    half = batch // 2
    rank = lax.axis_index("kvp")
    core = lax.rem(rank, 2)
    place = jnp.stack([core, rank, lax.axis_index("tp")]).astype(jnp.int32)
    partner = [(i, i ^ 1) for i in range(spread)]

    def swap(x):
        return lax.ppermute(x, "kvp", partner)

    def across(x):
        return [x] + [
            lax.ppermute(x, "kvp", [(i, (i + 2 * k) % spread) for i in range(spread)]) for k in range(1, chips)
        ]

    def chip_sum(other, mine):
        return across((mine + swap(other)).astype(BF16))

    tile = 256 if width % 256 == 0 else LANES
    q_parts = []
    for h in range(kv_local):
        q_parts.append(project(place, normed, [w_query], h * width, width, tile))
    kv_width = w_key.shape[1]
    kv_part = project(place, normed, [w_key, w_value], 0, kv_width, kv_width)

    position = lax.dynamic_slice_in_dim(lengths, core * half, half, 0).astype(F32)
    cosine, sine = angles(position, head_dim)
    owner, count = invert_table(place, page_table, lengths, pages, page, half)

    queries = []
    for h in range(kv_local):
        q_mine = rotate_sum(chip_sum(*q_parts[h]), cosine, sine, width)
        queries.append((q_mine, swap(q_mine)))
    kv_rows = rotate_sum(chip_sum(*kv_part), cosine, sine, kv_width)

    pieces = []
    for h in range(kv_local):
        q_mine, q_other = queries[h]
        mine, other = attend(q_mine, q_other, owner, count, key_cache, value_cache, h, scale)
        merged = across(pair_merge(mine, swap(other), group))
        out = finish(merged, q_mine, kv_rows, h, kv_local, scale)
        pieces.append((out, swap(out)))

    terms = project_out(place, pieces, w_out, batch // ways)
    total = terms[0]
    for k in range(1, ways):
        total = total + lax.ppermute(terms[k], "tp", [(i, (i + k) % ways) for i in range(ways)]).astype(F32)
    return total.astype(BF16)


def solution(mesh):
    return jax.shard_map(
        body,
        mesh=mesh,
        in_specs=(
            P("grp", "kvp"),
            P("kvp", "tp"),
            P("kvp", "tp"),
            P("kvp", "tp"),
            P("tp", "kvp"),
            P("tp", ("grp", "kvp"), None, None),
            P("tp", ("grp", "kvp"), None, None),
            P("grp"),
            P("grp", None),
        ),
        out_specs=P(("grp", "tp"), "kvp"),
        check_vma=False,
    )
```

```python
import functools

import jax
import jax.numpy as jnp
from jax import lax
from jax.experimental import pallas as pl
from jax.experimental.pallas import tpu as pltpu
from jax.sharding import PartitionSpec as P

ROPE_BASE = 1000000.0
NEG = -1e30
TWO_PI_HIGH = 6.28125
TWO_PI_LOW = 0.0019353071795864769
LANES = 128
F32 = jnp.float32
BF16 = jnp.bfloat16
MIB = 1024 * 1024


def angles(pos, width):
    half = width // 2
    freq = ROPE_BASE ** (-(2.0 * jnp.arange(half, dtype=F32)) / width)
    coarse = lax.optimization_barrier(freq.astype(BF16)).astype(F32)
    fine = freq - coarse
    pos_e = pos[..., None]
    exact = pos_e * coarse
    turns = jnp.floor(exact / TWO_PI_HIGH)
    angle = exact - turns * TWO_PI_HIGH - turns * TWO_PI_LOW + pos_e * fine
    cosine = jnp.cos(angle)
    sine = jnp.sin(angle)
    return jnp.concatenate([cosine, cosine], -1), jnp.concatenate([-sine, sine], -1)


def in_vmem():
    return pl.BlockSpec(memory_space=pltpu.VMEM)


def in_hbm():
    return pl.BlockSpec(memory_space=pltpu.HBM)


def params(mib):
    return pltpu.CompilerParams(vmem_limit_bytes=mib * MIB)


def core_index():
    return lax.rem(lax.axis_index("kvp"), 2)


def project_kernel(half, spans, tile, fetch, n_ref, *refs):
    count = len(spans)
    weights = refs[:count]
    other_ref, mine_ref = refs[count : count + 2]
    rows_ref = refs[count + 2] if fetch else n_ref
    buf, sem = refs[-2:]
    core = core_index()
    copies = []
    if fetch:
        for i, c in enumerate((1 - core, core)):
            copies.append(
                pltpu.make_async_copy(
                    n_ref.at[pl.ds(pl.multiple_of(c * half, half), half), :],
                    rows_ref.at[pl.ds(i * half, half), :],
                    sem.at[i],
                )
            )
    blocks = []
    column = 0
    for w_ref, (start, span) in zip(weights, spans):
        for at in range(0, span, tile):
            cols = slice(column, column + tile)
            copy = pltpu.make_async_copy(
                w_ref.at[:, pl.ds(start + at, tile)], buf.at[:, cols], sem.at[2 + len(blocks)]
            )
            blocks.append((cols, copy))
            column += tile
    for copy in copies + [copy for _, copy in blocks]:
        copy.start()
    for copy in copies:
        copy.wait()
    rows = rows_ref[...]
    for cols, copy in blocks:
        copy.wait()
        acc = jnp.dot(rows, buf[:, cols], preferred_element_type=F32)
        other_ref[:, cols] = acc[:half]
        mine_ref[:, cols] = acc[half:]


def project(normed, weights, spans, fetch):
    batch, depth = normed.shape
    half = batch // 2
    total = sum(span for _, span in spans)
    tile = 256 if all(span % 256 == 0 for _, span in spans) else LANES
    outs = [jax.ShapeDtypeStruct((half, total), F32)] * 2
    if fetch:
        outs.append(jax.ShapeDtypeStruct(normed.shape, normed.dtype))
    return pl.pallas_call(
        functools.partial(project_kernel, half, spans, tile, fetch),
        out_shape=outs,
        in_specs=[in_hbm() if fetch else in_vmem()] + [in_hbm()] * len(weights),
        out_specs=[in_vmem()] * len(outs),
        scratch_shapes=[
            pltpu.VMEM((depth, total), BF16),
            pltpu.SemaphoreType.DMA((2 + total // tile,)),
        ],
        compiler_params=params(8),
        cost_estimate=pl.CostEstimate(
            flops=2 * batch * depth * total,
            transcendentals=0,
            bytes_accessed=2 * depth * (batch + total) + 8 * half * total,
        ),
        name="project",
    )(normed, *weights)


def prepare_kernel(batch, half, pages, t_ref, c_ref, k_hbm, v_hbm, _, owner_ref, count_ref, k_ref, v_ref, sem):
    copies = [
        pltpu.make_async_copy(k_hbm.at[0], k_ref, sem.at[0]),
        pltpu.make_async_copy(v_hbm.at[0], v_ref, sem.at[1]),
    ]
    for copy in copies:
        copy.start()
    slot = lax.broadcasted_iota(jnp.int32, (pages, LANES), 0) + lax.axis_index("kvp") * pages

    def step(r, total):
        ids = t_ref[pl.ds(r * 8, 8), :]
        codes = c_ref[pl.ds(r * 8, 8), :]
        for k in range(8):
            total = total + jnp.where(ids[k : k + 1, :] == slot, codes[k : k + 1, :], 0)
        return total

    total = lax.fori_loop(0, t_ref.shape[0] // 8, step, jnp.zeros((pages, LANES), jnp.int32))
    code = jnp.sum(total, axis=1, keepdims=True)
    owner = lax.shift_right_logical(code, 8) - core_index() * half
    owner_ref[...] = jnp.where(owner < 0, owner + batch, owner)
    count_ref[...] = code & 255
    for copy in copies:
        copy.wait()


def prepare(page_table, lengths, key_cache, value_cache, half, after):
    pages, page, dim = key_cache.shape[1:]
    batch, blocks = page_table.shape
    left = lengths[:, None] - page * jnp.arange(blocks, dtype=jnp.int32)[None, :]
    code = jnp.arange(batch, dtype=jnp.int32)[:, None] * 256 + jnp.clip(left, 0, page)
    column = jax.ShapeDtypeStruct((pages, 1), jnp.int32)
    return pl.pallas_call(
        functools.partial(prepare_kernel, batch, half, pages),
        out_shape=(column, column) + (jax.ShapeDtypeStruct((pages, page, dim), key_cache.dtype),) * 2,
        in_specs=[in_vmem()] * 2 + [in_hbm()] * 2 + [pl.BlockSpec(memory_space=pl.ANY)],
        out_specs=[in_vmem()] * 4,
        scratch_shapes=[pltpu.SemaphoreType.DMA((2,))],
        compiler_params=params(4),
        name="prepare",
    )(page_table.reshape(-1, LANES), code.reshape(-1, LANES), key_cache, value_cache, after)


def rotate_kernel(count, plain, *refs):
    parts = refs[:count]
    cos_ref, sin_ref = refs[count : count + 2]
    outs = refs[count + 3 :]
    cosine = cos_ref[...]
    sine = sin_ref[...]
    at = 0
    for out_ref in outs:
        for start in range(0, out_ref.shape[1], LANES):
            cols = slice(at, at + LANES)
            x = parts[0][:, cols].astype(F32)
            for part in parts[1:]:
                x = x + part[:, cols].astype(F32)
            if at < plain:
                x = x * cosine + pltpu.roll(x, LANES // 2, 1) * sine
            out_ref[:, start : start + LANES] = x.astype(BF16)
            at += LANES


def rotate_sum(parts, cosine, sine, widths, plain, after):
    return pl.pallas_call(
        functools.partial(rotate_kernel, len(parts), plain),
        out_shape=[jax.ShapeDtypeStruct((parts[0].shape[0], width), BF16) for width in widths],
        in_specs=[in_vmem()] * (len(parts) + 2) + [pl.BlockSpec(memory_space=pl.ANY)],
        out_specs=[in_vmem()] * len(widths),
        compiler_params=params(4),
        name="rotate",
    )(*parts, cosine, sine, after)


def attend_kernel(group, scale, following, together, qm_ref, qo_ref, own_ref, cnt_ref, k_ref, v_ref, *refs):
    pages, page, dim = k_ref.shape
    copies = []
    if following is None:
        out_ref, q_sc = refs
    else:
        k_hbm, v_hbm, out_ref, k_next, v_next, q_sc, sem = refs
        copies = [
            pltpu.make_async_copy(k_hbm.at[following], k_next, sem.at[0]),
            pltpu.make_async_copy(v_hbm.at[following], v_next, sem.at[1]),
        ]
    for copy in copies:
        copy.start()
    half = qm_ref.shape[0]
    lane_row = lax.broadcasted_iota(jnp.int32, (pages, 2 * half), 1)
    pick = jnp.where(own_ref[...] == lane_row, 1.0, 0.0).astype(BF16)
    q_sc[...] = jnp.dot(pick[:, :half], qm_ref[...], preferred_element_type=F32) + jnp.dot(
        pick[:, half:], qo_ref[...], preferred_element_type=F32
    )
    sub = lax.broadcasted_iota(jnp.int32, (group * 8, LANES), 0) % 8
    lane = lax.broadcasted_iota(jnp.int32, (group * 8, LANES), 1)
    lane8 = lax.broadcasted_iota(jnp.int32, (8, LANES), 1)
    keep = [jnp.where(sub == k, 1.0, 0.0).astype(BF16) for k in range(8)]

    def step(it, carry):
        bases = [pl.multiple_of(it * (8 * together) + 8 * j, 8) for j in range(together)]
        raws = []
        for base in bases:
            q = jnp.concatenate(
                [q_sc[pl.ds(base, 8), h * LANES : (h + 1) * LANES] for h in range(group)], axis=0
            ).astype(BF16)
            keys = k_ref[pl.ds(base, 8)].reshape(8 * page, dim)
            raw = lax.dot_general(q, keys, (((1,), (1,)), ((), ())), preferred_element_type=F32)
            s = raw[:, :LANES]
            for k in range(1, 8):
                s = jnp.where(sub == k, raw[:, k * LANES : (k + 1) * LANES], s)
            raws.append(s)
        soft = []
        for base, s in zip(bases, raws):
            count = jnp.concatenate([cnt_ref[pl.ds(base, 8), :]] * group, axis=0)
            valid = lane < count
            s = jnp.where(valid, s * scale, NEG)
            top = jnp.max(s, axis=1, keepdims=True)
            w = jnp.where(valid, jnp.exp(s - top), 0.0)
            total = jnp.sum(w, axis=1, keepdims=True)
            soft.append((count > 0, top, total, w.astype(BF16)))
        for base, (some, top, total, w) in zip(bases, soft):
            values = v_ref[pl.ds(base, 8)].reshape(8 * page, dim)
            spread = jnp.concatenate([w * mask for mask in keep], axis=1)
            out = jnp.dot(spread, values, preferred_element_type=F32)
            safe = jnp.where(some, total, 1.0)
            out = jnp.where(some, out / safe, 0.0)
            lse = jnp.where(some, top + jnp.log(safe), NEG)
            packed = jnp.where(lane8 == 8, own_ref[pl.ds(base, 8), :].astype(F32), NEG)
            for h in range(group):
                out_ref[pl.ds(base, 8), h * LANES : (h + 1) * LANES] = out[h * 8 : (h + 1) * 8]
                packed = jnp.where(lane8 == h, lse[h * 8 : (h + 1) * 8], packed)
            out_ref[pl.ds(base, 8), group * LANES :] = packed
        return carry

    lax.fori_loop(0, pages // (8 * together), step, 0)
    for copy in copies:
        copy.wait()


def attend(q_mine, q_other, owner, count, keys, values, key_cache, value_cache, head, scale):
    half, width = q_mine.shape
    group = width // LANES
    pages, page, dim = key_cache.shape[1:]
    together = 4 if pages % 32 == 0 else 1
    more = head + 1 < key_cache.shape[0]
    slots = jax.ShapeDtypeStruct((pages, width + LANES), F32)
    loaded = jax.ShapeDtypeStruct((pages, page, dim), key_cache.dtype)
    return pl.pallas_call(
        functools.partial(attend_kernel, group, scale, head + 1 if more else None, together),
        out_shape=[slots] + [loaded] * (2 * more),
        in_specs=[in_vmem()] * 6 + [in_hbm()] * (2 * more),
        out_specs=[in_vmem()] * (1 + 2 * more),
        scratch_shapes=[pltpu.VMEM((pages, width), F32)] + [pltpu.SemaphoreType.DMA((2,))] * more,
        compiler_params=params(6),
        cost_estimate=pl.CostEstimate(
            flops=4 * pages * page * dim * group * 8,
            transcendentals=pages * page * group,
            bytes_accessed=4 * pages * page * dim,
        ),
        name="attend",
    )(q_mine, q_other, owner, count, keys, values, *((key_cache, value_cache) if more else ()))


def three_parts(x):
    high = x.astype(BF16)
    rest = x - high.astype(F32)
    middle = rest.astype(BF16)
    return high, middle, (rest - middle.astype(F32)).astype(BF16)


def merge_kernel(group, a_ref, b_ref, out_ref):
    pages = a_ref.shape[0]
    half = out_ref.shape[0]
    extra = slice(group * LANES, (group + 1) * LANES)
    small = jnp.concatenate([a_ref[:, extra], b_ref[:, extra]], axis=0)
    place = small[:, 8:9].astype(jnp.int32)
    first = lax.broadcasted_iota(jnp.int32, (2 * pages, 1), 0) < pages
    place = jnp.where(first, place, place - half)
    row = lax.broadcasted_iota(jnp.int32, (2 * pages, half), 1)
    mask = (place == row) & (small[:, 0:1] > 0.5 * NEG)
    pick = jnp.where(mask, 1.0, 0.0).astype(BF16)
    tops = []
    for h in range(group):
        tops.append(jnp.max(jnp.where(mask, small[:, h : h + 1], NEG), axis=0, keepdims=True))
    tops.append(jnp.full((LANES - group, half), NEG, F32))
    top = jnp.concatenate(tops, axis=0).T
    back = jnp.dot(pick, jnp.concatenate(three_parts(top), axis=1), preferred_element_type=F32)
    back = back[:, :LANES] + back[:, LANES : 2 * LANES] + back[:, 2 * LANES :]
    lane = lax.broadcasted_iota(jnp.int32, small.shape, 1)
    weight = jnp.where(lane < group, jnp.exp(jnp.minimum(small - back, 0.0)), 0.0).astype(BF16)
    flip = (((0,), (0,)), ((), ()))
    total = lax.dot_general(pick, weight, flip, preferred_element_type=F32)
    safe = jnp.where(total > 0.0, total, 1.0)
    inverse = 1.0 / safe
    wide = weight.astype(F32)
    for h in range(group):
        cols = slice(h * LANES, (h + 1) * LANES)
        scaled = jnp.concatenate(
            [a_ref[:, cols] * wide[:pages, h : h + 1], b_ref[:, cols] * wide[pages:, h : h + 1]], axis=0
        ).astype(BF16)
        rows = lax.dot_general(pick, scaled, flip, preferred_element_type=F32)
        out_ref[:, cols] = (rows * inverse[:, h : h + 1]).astype(BF16)
    lse = jnp.where(total > 0.0, top + jnp.log(safe), NEG)
    high, middle, low = [x.astype(F32) for x in three_parts(lse)]
    lane = lax.broadcasted_iota(jnp.int32, lse.shape, 1)
    packed = jnp.where(lane < 8, high, 0.0)
    packed = jnp.where((lane >= 8) & (lane < 16), pltpu.roll(middle, 8, 1), packed)
    packed = jnp.where((lane >= 16) & (lane < 24), pltpu.roll(low, 16, 1), packed)
    out_ref[:, extra] = packed.astype(BF16)


def merge(a, b, half):
    return pl.pallas_call(
        functools.partial(merge_kernel, a.shape[1] // LANES - 1),
        out_shape=jax.ShapeDtypeStruct((half, a.shape[1]), BF16),
        in_specs=[in_vmem()] * 2,
        out_specs=in_vmem(),
        compiler_params=params(6),
        name="merge",
    )(a, b)


def finish_kernel(group, scale, head, kv_local, *refs):
    q_ref, kv_ref, out_ref = refs[-3:]
    parts = refs[:-3]
    keys = kv_ref[:, head * LANES : (head + 1) * LANES].astype(F32)
    values = kv_ref[:, (kv_local + head) * LANES : (kv_local + head + 1) * LANES].astype(F32)
    lses = []
    for part in parts:
        x = part[:, group * LANES :].astype(F32)
        lses.append(x + pltpu.roll(x, LANES - 8, 1) + pltpu.roll(x, LANES - 16, 1))
    for h in range(group):
        cols = slice(h * LANES, (h + 1) * LANES)
        s_new = jnp.sum(q_ref[:, cols].astype(F32) * keys, axis=1, keepdims=True) * scale
        top = s_new
        for lse in lses:
            top = jnp.maximum(top, lse[:, h : h + 1])
        w_new = jnp.exp(s_new - top)
        total = w_new
        acc = w_new * values
        for part, lse in zip(parts, lses):
            w = jnp.exp(lse[:, h : h + 1] - top)
            total = total + w
            acc = acc + w * part[:, cols].astype(F32)
        out_ref[:, cols] = (acc / total).astype(BF16)


def finish(parts, q_mine, kv_rows, head, kv_local, scale):
    group = q_mine.shape[1] // LANES
    return pl.pallas_call(
        functools.partial(finish_kernel, group, scale, head, kv_local),
        out_shape=jax.ShapeDtypeStruct(q_mine.shape, BF16),
        in_specs=[in_vmem()] * (len(parts) + 2),
        out_specs=in_vmem(),
        compiler_params=params(4),
        name="finish",
    )(*parts, q_mine, kv_rows)


def output_kernel(rows, heads, tile, *refs):
    ins = refs[: 2 * heads]
    w_ref = refs[2 * heads]
    outs = refs[2 * heads + 1 : -1]
    x_sc = refs[-1]
    batch = x_sc.shape[0]
    half = batch // 2
    core = core_index()
    me = lax.axis_index("tp")
    width = ins[0].shape[1]
    ways = batch // rows
    for h in range(heads):
        cols = slice(h * width, (h + 1) * width)
        x_sc[pl.ds(pl.multiple_of(core * half, half), half), cols] = ins[2 * h][...]
        x_sc[pl.ds(pl.multiple_of((1 - core) * half, half), half), cols] = ins[2 * h + 1][...]
    x = jnp.concatenate(
        [x_sc[pl.ds(pl.multiple_of(lax.rem(me + k, ways) * rows, rows), rows), :] for k in range(ways)], axis=0
    )
    for at in range(0, w_ref.shape[1], tile):
        cols = slice(at, at + tile)
        acc = jnp.dot(x, w_ref[:, cols], preferred_element_type=F32)
        for k, out in enumerate(outs):
            out[:, cols] = acc[k * rows : (k + 1) * rows].astype(out.dtype)


def project_out(pieces, w_out, rows):
    heads = len(pieces)
    half, width = pieces[0][0].shape
    batch = 2 * half
    depth, columns = w_out.shape
    tile = 256 if columns % 256 == 0 else LANES
    ways = batch // rows
    return pl.pallas_call(
        functools.partial(output_kernel, rows, heads, tile),
        out_shape=[jax.ShapeDtypeStruct((rows, columns), F32 if k == 0 else BF16) for k in range(ways)],
        in_specs=[in_vmem()] * (2 * heads + 1),
        out_specs=[in_vmem()] * ways,
        scratch_shapes=[pltpu.VMEM((batch, depth), BF16)],
        compiler_params=params(8),
        cost_estimate=pl.CostEstimate(
            flops=2 * batch * depth * columns, transcendentals=0, bytes_accessed=2 * depth * columns + 2 * batch * columns
        ),
        name="project_out",
    )(*[x for piece in pieces for x in piece], w_out)


def add_kernel(*refs):
    total = refs[0][...].astype(F32)
    for ref in refs[1:-1]:
        total = total + ref[...].astype(F32)
    refs[-1][...] = total.astype(refs[-1].dtype)


def add(*terms):
    return pl.pallas_call(
        add_kernel,
        out_shape=jax.ShapeDtypeStruct(terms[0].shape, BF16),
        in_specs=[in_vmem()] * len(terms),
        out_specs=in_vmem(),
        compiler_params=params(4),
        name="add",
    )(*terms)


def reduce_scatter(terms):
    ways = len(terms)
    spread = lax.axis_size("kvp")

    def move(x, k):
        return lax.ppermute(x, "tp", [(i, (i + k) % ways) for i in range(ways)])

    if ways != 4:
        return add(terms[0], *[move(terms[k], k) for k in range(1, ways)])
    pairs = []
    for i in range(spread):
        for j in range(ways):
            pairs.append((i * ways + j, i * ways + (j + (1 if i % 2 == 0 else 3)) % ways))
    passed = lax.ppermute(terms[2], ("kvp", "tp"), pairs)
    up, down = route(terms[1], terms[3], passed)
    return add(terms[0], move(up, 1), move(down, 3))


def route_kernel(up_ref, down_ref, passed_ref, up_out, down_out):
    passed = passed_ref[...].astype(F32)
    first = lax.broadcasted_iota(jnp.int32, passed.shape, 0) * 0 + core_index() == 0
    up_out[...] = (up_ref[...].astype(F32) + jnp.where(first, passed, 0.0)).astype(BF16)
    down_out[...] = (down_ref[...].astype(F32) + jnp.where(first, 0.0, passed)).astype(BF16)


def route(up, down, passed):
    return pl.pallas_call(
        route_kernel,
        out_shape=[jax.ShapeDtypeStruct(up.shape, BF16)] * 2,
        in_specs=[in_vmem()] * 3,
        out_specs=[in_vmem()] * 2,
        compiler_params=params(4),
        name="route",
    )(up, down, passed)


def body(normed, w_query, w_key, w_value, w_out, key_cache, value_cache, lengths, page_table):
    normed, w_query, w_key, w_value, key_cache, value_cache = (
        pltpu.with_memory_space_constraint(x, pltpu.HBM)
        for x in (normed, w_query, w_key, w_value, key_cache, value_cache)
    )
    batch = normed.shape[0]
    kv_local, pages, page, head_dim = key_cache.shape
    group = w_query.shape[1] // (kv_local * head_dim)
    width = group * head_dim
    scale = head_dim ** (-0.5)
    spread = lax.axis_size("kvp")
    ways = lax.axis_size("tp")
    chips = spread // 2
    half = batch // 2
    core = core_index()
    partner = [(i, i ^ 1) for i in range(spread)]

    def swap(x):
        return lax.ppermute(x, "kvp", partner)

    def across(x):
        return [x] + [
            lax.ppermute(x, "kvp", [(i, (i + 2 * k) % spread) for i in range(spread)]) for k in range(1, chips)
        ]

    def chip_sum(other, mine):
        return across((mine + swap(other)).astype(BF16))

    kv_width = w_key.shape[1]
    q_parts = []
    rows = normed
    for h in range(kv_local):
        weights, spans = [w_query], [(h * width, width)]
        if h == kv_local - 1:
            weights += [w_key, w_value]
            spans += [(0, kv_width)] * 2
        other, mine, *brought = project(rows, weights, spans, h == 0)
        if brought:
            rows = brought[0]
        q_parts.append(chip_sum(other, mine))

    position = lax.dynamic_slice_in_dim(lengths, core * half, half, 0).astype(F32)
    cosine, sine = angles(position, head_dim)
    owner, count, keys, values = prepare(page_table, lengths, key_cache, value_cache, half, q_parts[-1][0])

    after = keys
    queries = []
    slots = []
    for h in range(kv_local):
        last = h == kv_local - 1
        q_mine, *rest = rotate_sum(
            q_parts[h], cosine, sine, [width, 2 * kv_width] if last else [width], width + kv_width, after
        )
        if last:
            kv_rows = rest[0]
        queries.append(q_mine)
        after, *loaded = attend(
            q_mine, swap(q_mine), owner, count, keys, values, key_cache, value_cache, h, scale
        )
        slots.append(after)
        if loaded:
            keys, values = loaded
    pieces = []
    for h in range(kv_local):
        merged = across(merge(slots[h], swap(slots[h]), half))
        out = finish(merged, queries[h], kv_rows, h, kv_local, scale)
        pieces.append((out, swap(out)))

    terms = project_out(pieces, w_out, batch // ways)
    return reduce_scatter(terms)


def solution(mesh):
    return jax.shard_map(
        body,
        mesh=mesh,
        in_specs=(
            P("grp", "kvp"),
            P("kvp", "tp"),
            P("kvp", "tp"),
            P("kvp", "tp"),
            P("tp", "kvp"),
            P("tp", ("grp", "kvp"), None, None),
            P("tp", ("grp", "kvp"), None, None),
            P("grp"),
            P("grp", None),
        ),
        out_specs=P(("grp", "tp"), "kvp"),
        check_vma=False,
    )
```
